32 devices in a mesh: groups: 2 (over y), blk: 4 (over z), dp: 2 (over x), sub: 2 (over core).
Axes of the slice: x: 2, y: 2, z: 4, core: 2. Of those that a mesh axis runs over, the one named last changes fastest.
Arguments:
- view_a: bfloat16 [2048, 256], P(('groups', 'blk', 'dp', 'sub')), parts along dimension 0, may hold values from -6 to 6
- view_b: bfloat16 [2048, 256], P(('groups', 'blk', 'dp', 'sub')), parts along dimension 0, may hold values from -6 to 6
- prototypes: bfloat16 [32768, 256], P('blk'), may hold values from -6 to 6
- tile_mask: int32 [16, 256], replicated, may hold values from 0 to 1, as said below
- tile_region: int32 [32], P('groups'), parts along dimension 0, may hold values from 0 to 15, as said below
Outputs:
- grad_view_b: float32 [2048, 256], P(('groups', 'blk', 'dp', 'sub')), parts along dimension 0
- grad_prototypes: float32 [65536, 256], P(('groups', 'blk', 'dp', 'sub')), parts along dimension 0
The draws below stay inside these ranges and needn't reach their ends.
There are 2 independent parts, one for each index of `groups`. The reference program is written for one: setup_inputs(seed, part) draws one part's arguments, and reference() takes and returns one part's arrays. A program takes and returns all parts, laid end to end along the dimension named above; an argument that names none is the same for every part. Nothing has to cross between parts.
Inputs may be any that keep to these rules, and one draw needn't show every extreme that they name: `tile_mask`: every prototype tile is 1 for at least one region, and every region for at least 16 tiles. `tile_region`: every region is named by at least one hit tile.
All inputs are finite; a program needn't handle non-finite values.
Results may differ from the reference program's by a relative error of at most 0.00045.
The reference program's roundings to bfloat16 on the way count: a program that leaves them out, or rounds other values in their place, can miss the bound.
Values may be sent and summed in bfloat16 or wider, within the bound.
A program may use at most 64 MiB of HBM per device.

```python
import jax
import jax.numpy as jnp
from jax import lax

D = 256
K = 32768
TILE = 128
REGIONS = 16
ITERS = 3
HIT_DEV = 64
HIT_TILES = 16
HITS = 1024
KT = 256


def draw_tile_mask(key, part):
    first_key, second_key = jax.random.split(key)
    shuffled = jax.random.permutation(first_key, KT)
    homes = shuffled % REGIONS
    region_ids = jnp.arange(REGIONS, dtype=jnp.int32)
    home_flags = homes[None, :] == region_ids[:, None]
    extra_bits = jax.random.randint(second_key, (REGIONS, KT), 0, 4) == 0
    return jnp.logical_or(home_flags, extra_bits).astype(jnp.int32)


def draw_tile_region(key, part):
    shuffled = jax.random.permutation(key, HIT_TILES)
    return (shuffled % REGIONS).astype(jnp.int32)


def block_scale(key, extent, cuts, smallest, top_value):
    def one(position, shards_of):
        draws = jax.random.uniform(jax.random.fold_in(jax.random.fold_in(key, 6), position), (shards_of,), jnp.float32, smallest / len(cuts), top_value / len(cuts))
        return jnp.repeat(jnp.exp(draws), extent[position] // shards_of).reshape((-1,) + (1,) * (len(extent) - position - 1))

    gain = one(*cuts[0])
    for cut in cuts[1:]:
        gain = gain * one(*cut)
    return gain


def normal_values(key, shape, width, reach, cuts=(), held_as=jnp.bfloat16):
    gain = block_scale(key, shape, cuts, -0.22, 0.18) if cuts else 1.0
    values = jax.random.normal(key, shape, jnp.float32) * width * gain
    return jnp.minimum(jnp.maximum(values, -reach), reach).astype(held_as)


def setup_inputs(seed: int = 0, part: int = 0) -> dict:
    streams_of = jax.random.split(jax.random.key(seed), 6)
    part_splits = jax.random.split(jax.random.fold_in(streams_of[5], part), 6)
    return {
        "view_a": normal_values(part_splits[0], (HITS, D), 1.0, 6.0, ((0, 16),)),
        "view_b": normal_values(part_splits[1], (HITS, D), 1.0, 6.0, ((0, 16),)),
        "prototypes": normal_values(streams_of[2], (K, D), 1.0, 6.0, ((0, 4),)),
        "tile_mask": draw_tile_mask(jax.random.fold_in(streams_of[5], 71), part),
        "tile_region": draw_tile_region(jax.random.fold_in(jax.random.fold_in(streams_of[5], part), 71), part),
    }


SOFTMAX_TEMPER = 0.1
EPSILON = 0.05

def unit_rows(matrix):
    values = matrix.astype(jnp.float32)
    return (values * lax.rsqrt(lax.optimization_barrier(jnp.sum(values * values, axis=1, keepdims=True)) + 1e-06)).astype(jnp.bfloat16)

def reference(view_a, view_b, prototypes, tile_mask, tile_region):
    unit_a = unit_rows(view_a)
    unit_b = unit_rows(view_b)
    unit_protos = unit_rows(prototypes)
    block_cols = min(K, 1024)
    block_count = K // block_cols
    region_rows = jnp.repeat(tile_region, HIT_DEV)
    row_tiles = tile_mask[region_rows]
    block_ids = jnp.arange(block_count, dtype=jnp.int32)

    def block_pieces(block_index):
        col_block = lax.dynamic_slice_in_dim(unit_protos, (block_index * block_cols).astype(jnp.int32), block_cols, 0)
        flags = lax.dynamic_slice_in_dim(row_tiles, (block_index * (block_cols // TILE)).astype(jnp.int32), block_cols // TILE, 1)
        return (col_block, jnp.repeat(flags > 0, TILE, axis=1))

    def codes_block(block_index):
        col_block, live_block_mask = block_pieces(block_index)
        prototype_scores = jnp.dot(unit_a, col_block.T, preferred_element_type=jnp.float32)
        code_exp = jnp.where(live_block_mask, jnp.exp((prototype_scores - 1.0) / EPSILON), 0.0).astype(jnp.bfloat16)
        return lax.optimization_barrier(code_exp).astype(jnp.float32)

    def balancing_sweep(row_inverses):

        def pass_turn(running, block_index):
            code_exp = codes_block(block_index)
            column_inverses = 1.0 / lax.optimization_barrier(jnp.sum(code_exp * row_inverses[:, None], axis=0))
            return (running + lax.optimization_barrier(jnp.sum(code_exp * column_inverses[None, :], axis=1)), column_inverses)
        row_totals, column_inverses = lax.scan(pass_turn, jnp.zeros((HITS,), jnp.float32), block_ids)
        return (1.0 / row_totals, column_inverses.reshape(-1))

    def norm_turn(running, block_index):
        col_block, live_block_mask = block_pieces(block_index)
        prototype_scores = jnp.dot(unit_b, col_block.T, preferred_element_type=jnp.float32)
        prototype_weights = jnp.where(live_block_mask, jnp.exp((prototype_scores - 1.0) / SOFTMAX_TEMPER), 0.0)
        return (running + lax.optimization_barrier(jnp.sum(prototype_weights, axis=1)), None)
    second_view_norm, unused = lax.scan(norm_turn, jnp.zeros((HITS,), jnp.float32), block_ids)
    row_inverses = jnp.ones((HITS,), jnp.float32)
    column_inverses = jnp.ones((K,), jnp.float32)
    for sweep_index in range(ITERS):
        row_inverses, column_inverses = balancing_sweep(row_inverses)

    def grad_turn(running, block_index):
        col_block, live_block_mask = block_pieces(block_index)
        code_exp = codes_block(block_index)
        prototype_scores = jnp.dot(unit_b, col_block.T, preferred_element_type=jnp.float32)
        predicted_logits = jnp.where(live_block_mask, jnp.exp((prototype_scores - 1.0) / SOFTMAX_TEMPER), 0.0) / second_view_norm[:, None]
        recip_block = lax.dynamic_slice_in_dim(column_inverses, (block_index * block_cols).astype(jnp.int32), block_cols, 0)
        code_entries = row_inverses[:, None] * code_exp * recip_block[None, :]
        score_gradient = ((predicted_logits - code_entries) / SOFTMAX_TEMPER).astype(jnp.bfloat16)
        hit_part = jnp.dot(score_gradient, col_block, preferred_element_type=jnp.float32)
        proto_part = jnp.dot(score_gradient.T, unit_b, preferred_element_type=jnp.float32)
        return (running + hit_part, proto_part)
    grad_view_b, proto_parts = lax.scan(grad_turn, jnp.zeros((HITS, D), jnp.float32), block_ids)
    return (grad_view_b, proto_parts.reshape(K, D))
```

```python
import jax
import jax.numpy as jnp
from jax import lax
from jax.sharding import PartitionSpec as P

TILE = 128
ITERS = 3
SOFTMAX_TEMPER = 0.1
EPSILON = 0.05
PART = ("blk", "dp", "sub")


def unit_rows(matrix):
    values = matrix.astype(jnp.float32)
    return (values * lax.rsqrt(jnp.sum(values * values, axis=1, keepdims=True) + 1e-06)).astype(
        jnp.bfloat16
    )


def body(view_a, view_b, prototypes, tile_mask, tile_region):
    n_dp = lax.axis_size("dp")
    n_sub = lax.axis_size("sub")
    blk_pos = lax.axis_index("blk")
    inner_pos = lax.axis_index("dp") * n_sub + lax.axis_index("sub")
    hit_dev, width = view_a.shape
    cols = prototypes.shape[0] // (n_dp * n_sub)
    tiles = cols // TILE
    regions = tile_mask.shape[0]
    protos = unit_rows(lax.dynamic_slice_in_dim(prototypes, inner_pos * cols, cols, 0))
    both = jnp.concatenate([unit_rows(view_a), unit_rows(view_b)], axis=1)
    both = lax.all_gather(both, PART, axis=0, tiled=True)
    rows_a, rows_b = both[:, :width], both[:, width:]
    hits = rows_a.shape[0]
    own_tile = (blk_pos * n_dp * n_sub + inner_pos) * tiles
    my_mask = lax.dynamic_slice_in_dim(tile_mask, own_tile, tiles, 1).astype(jnp.float32)
    onehot = (tile_region[:, None] == jnp.arange(regions, dtype=jnp.int32)[None, :]).astype(
        jnp.float32
    )
    flags = jnp.dot(onehot, my_mask) > 0.5
    active = jnp.broadcast_to(
        flags[:, None, :, None], (hits // hit_dev, hit_dev, tiles, TILE)
    ).reshape(hits, cols)

    def scores(rows):
        return jnp.einsum("rd,kd->rk", rows, protos, preferred_element_type=jnp.float32)

    code_exp = jnp.where(active, jnp.exp((scores(rows_a) - 1.0) / EPSILON), 0.0).astype(
        jnp.bfloat16
    )
    pred = jnp.where(active, jnp.exp((scores(rows_b) - 1.0) / SOFTMAX_TEMPER), 0.0)
    norm = jnp.sum(pred, axis=1)
    code = code_exp.astype(jnp.float32)
    row = jnp.ones((hits,), jnp.float32)
    for sweep in range(ITERS):
        col = 1.0 / jnp.sum(code * row[:, None], axis=0)
        part = jnp.sum(code * col[None, :], axis=1)
        if sweep == 0:
            part, norm = lax.psum((part, norm), PART)
        else:
            part = lax.psum(part, PART)
        row = 1.0 / part
    grad = (
        (pred / norm[:, None] - row[:, None] * code * col[None, :]) / SOFTMAX_TEMPER
    ).astype(jnp.bfloat16)
    hit_part = jnp.dot(grad, protos, preferred_element_type=jnp.float32)
    grad_protos = jnp.einsum("rk,rd->kd", grad, rows_b, preferred_element_type=jnp.float32)
    return (lax.psum_scatter(hit_part, PART, scatter_dimension=0, tiled=True), grad_protos)


def solution(mesh):
    spread = P(("groups", "blk", "dp", "sub"), None)
    return jax.shard_map(
        body,
        mesh=mesh,
        in_specs=(spread, spread, P("blk", None), P(), P("groups")),
        out_specs=(spread, spread),
        check_vma=False,
    )
```

```python
import functools
import math

import jax
import jax.numpy as jnp
from jax import lax
from jax.experimental import pallas as pl
from jax.experimental.pallas import tpu as pltpu
from jax.sharding import PartitionSpec as P

TILE = 128
ITERS = 3
SOFTMAX_TEMPER = 0.1
EPSILON = 0.05
LOG2E = math.log2(math.e)
CODE_GAIN = LOG2E / EPSILON
PRED_GAIN = LOG2E / SOFTMAX_TEMPER
OFF = -1e30
MESH = pl.DeviceIdType.MESH
F32 = jnp.float32
BF16 = jnp.bfloat16


def unit_rows(matrix):
    values = matrix.astype(F32)
    return (values * lax.rsqrt(jnp.sum(values * values, axis=1, keepdims=True) + 1e-06)).astype(
        BF16
    )


def down_rows(row):
    return jnp.broadcast_to(row, (TILE, TILE)).T


def across_lanes(block):
    return jnp.sum(block.T, axis=0, keepdims=True)


def fold(block):
    return jnp.sum(block.reshape(block.shape[0] // 8, 8, block.shape[1]), axis=0)


def kernel(
    n_blk,
    n_dp,
    hit_dev,
    cols,
    region_ref,
    mask_ref,
    view_a_ref,
    view_b_ref,
    protos_ref,
    gview_ref,
    gproto_ref,
    rows_a,
    rows_b,
    protos,
    code,
    pred,
    lanes,
    colacc,
    colinv,
    rowinv,
    norminv,
    plane_msg,
    line_msg,
    hits2,
    red,
    s_in,
    x_in,
    z_out,
    z_in,
    load_sem,
    agz_send,
    agz_recv,
    agx_send,
    agx_recv,
    ags_send,
    ags_recv,
    arp_send,
    arp_recv,
    arz_send,
    arz_recv,
    rss_send,
    rss_recv,
    rsx_send,
    rsx_recv,
    rsz_send,
    rsz_recv,
):
    z = lax.axis_index("blk")
    x = lax.axis_index("dp")
    c = lax.axis_index("sub")
    plane = 2 * n_dp
    q = x * 2 + c
    group_rows = plane * hit_dev
    pairs = n_blk * n_dp
    tiles = cols // TILE
    first_tile = (z * plane + q) * tiles
    width = protos.shape[1]
    CC = min(256, cols)
    ctiles = CC // TILE

    barrier = pltpu.get_barrier_semaphore()

    def plane_id(step):
        other = lax.rem(q + step, plane)
        return {"dp": lax.div(other, 2), "sub": lax.rem(other, 2)}

    def line_id(step):
        return {"blk": lax.rem(z + step, n_blk)}

    for step in range(1, plane):
        pl.semaphore_signal(barrier, inc=1, device_id=plane_id(step), device_id_type=MESH)
    for step in range(1, n_blk):
        pl.semaphore_signal(barrier, inc=1, device_id=line_id(step), device_id_type=MESH)

    load = pltpu.make_async_copy(protos_ref.at[pl.ds(q * cols, cols)], protos, load_sem)
    load.start()
    rows_a[z, x, c] = unit_rows(view_a_ref[...])
    rows_b[z, x, c] = unit_rows(view_b_ref[...])
    pl.semaphore_wait(barrier, plane - 1 + n_blk - 1)

    sends = []

    def send(src, dst, send_sem, recv_sem, device):
        copy = pltpu.make_async_remote_copy(
            src_ref=src,
            dst_ref=dst,
            send_sem=send_sem,
            recv_sem=recv_sem,
            device_id=device,
            device_id_type=MESH,
        )
        copy.start()
        sends.append(copy)
        return copy

    def arrive(dst, send_sem, recv_sem, device):
        pltpu.make_async_remote_copy(
            src_ref=dst,
            dst_ref=dst,
            send_sem=send_sem,
            recv_sem=recv_sem,
            device_id=device,
            device_id_type=MESH,
        ).wait_recv()

    sub_id = {"sub": 1 - c}

    def source(k):
        return lax.rem(z - k + n_blk, n_blk)

    def near(dx):
        return lax.rem(x - dx + n_dp, n_dp)

    def to_sub(v, rows, k, dx):
        ref = rows.at[source(k), near(dx), c]
        send(ref, ref, ags_send.at[v, k, dx], ags_recv.at[v, k, dx], sub_id)

    def gather_a(v, rows, k):
        ref = rows.at[source(k), x, c]
        if k == 0:
            for step in range(1, n_blk):
                send(ref, ref, agz_send.at[v, step], agz_recv.at[v, step], line_id(step))
        else:
            arrive(ref, agz_send.at[v, k], agz_recv.at[v, k], line_id(k))
        for dx in range(1, n_dp):
            send(
                ref,
                ref,
                agx_send.at[v, k, dx],
                agx_recv.at[v, k, dx],
                {"dp": lax.rem(x + dx, n_dp)},
            )
        to_sub(v, rows, k, 0)

    def gather_b(v, rows, k):
        for dx in range(1, n_dp):
            ref = rows.at[source(k), near(dx), c]
            arrive(
                ref,
                agx_send.at[v, k, dx],
                agx_recv.at[v, k, dx],
                {"dp": lax.rem(x + dx, n_dp)},
            )
            to_sub(v, rows, k, dx)

    def gather_c(v, rows, k):
        for dx in range(n_dp):
            ref = rows.at[source(k), near(dx), 1 - c]
            arrive(ref, ags_send.at[v, k, dx], ags_recv.at[v, k, dx], sub_id)

    def bias(pair, core, tile, gain):
        region = region_ref[pair * 2 + core]
        return jnp.where(mask_ref[region, first_tile + tile] > 0, -gain, OFF).astype(F32)

    def score(rows, zi, xs, count, col):
        left = rows[zi, pl.ds(xs, count)].reshape(count * 2 * hit_dev, width)
        right = protos[pl.ds(col, CC), :]
        return lax.dot_general(
            left, right, (((1,), (1,)), ((), ())), preferred_element_type=F32
        )

    PX = min(2, n_dp)

    def code_group(k):
        zi = source(k)

        def step(t, carry):
            xs = (t % (n_dp // PX)) * PX
            ci = t // (n_dp // PX)
            col = pl.multiple_of(ci * CC, CC)
            s = score(rows_a, zi, xs, PX, col)
            for j in range(ctiles):
                total = None
                lane = pl.ds(pl.multiple_of(col + j * TILE, TILE), TILE)
                for i in range(PX):
                    for core in range(2):
                        lo = (i * 2 + core) * hit_dev
                        piece = s[lo : lo + hit_dev, j * TILE : (j + 1) * TILE]
                        b = bias(zi * n_dp + xs + i, core, ci * ctiles + j, CODE_GAIN)
                        e = jnp.exp2(piece * CODE_GAIN + b).astype(BF16)
                        row = pl.multiple_of(zi * group_rows + xs * 2 * hit_dev + lo, hit_dev)
                        code[pl.ds(row, hit_dev), lane] = e
                        part = fold(e.astype(F32))
                        total = part if total is None else total + part
                colacc[:, lane] = colacc[:, lane] + total
            return carry

        lax.fori_loop(0, (n_dp // PX) * (cols // CC), step, 0)

    def pred_group(zi):
        def block(t, carry):
            xs = t * PX
            lanes[...] = jnp.zeros_like(lanes)

            def step(ci, inner):
                col = pl.multiple_of(ci * CC, CC)
                s = score(rows_b, zi, xs, PX, col)
                for i in range(PX):
                    for core in range(2):
                        lo = (i * 2 + core) * hit_dev
                        total = None
                        for j in range(ctiles):
                            piece = s[lo : lo + hit_dev, j * TILE : (j + 1) * TILE]
                            b = bias(zi * n_dp + xs + i, core, ci * ctiles + j, PRED_GAIN)
                            e = jnp.exp2(piece * PRED_GAIN + b)
                            row = pl.multiple_of(
                                zi * group_rows + xs * 2 * hit_dev + lo, hit_dev
                            )
                            lane = pl.ds(pl.multiple_of(col + j * TILE, TILE), TILE)
                            pred[pl.ds(row, hit_dev), lane] = e
                            total = e if total is None else total + e
                        lanes[lo : lo + hit_dev, :] = lanes[lo : lo + hit_dev, :] + total
                return inner

            lax.fori_loop(0, cols // CC, step, 0)
            for i in range(PX):
                norminv[pl.ds(zi * n_dp + xs + i, 1), :] = across_lanes(
                    lanes[i * TILE : (i + 1) * TILE, :]
                )
            return carry

        lax.fori_loop(0, n_dp // PX, block, 0)

    def close_columns():
        total = jnp.sum(colacc[...], axis=0, keepdims=True)
        colinv[...] = jnp.broadcast_to(1.0 / total, colinv.shape)

    def column_pass():
        colacc[...] = jnp.zeros_like(colacc)

        def step(p, carry):
            scale = down_rows(rowinv[pl.ds(p, 1), :])
            row = pl.ds(pl.multiple_of(p * TILE, TILE), TILE)
            for j in range(tiles):
                lane = slice(j * TILE, (j + 1) * TILE)
                colacc[:, lane] = colacc[:, lane] + fold(code[row, lane].astype(F32) * scale)
            return carry

        lax.fori_loop(0, pairs, step, 0)
        close_columns()

    def row_pass(sweep):
        def step(p, carry):
            row = pl.ds(pl.multiple_of(p * TILE, TILE), TILE)
            total = None
            for j in range(tiles):
                lane = slice(j * TILE, (j + 1) * TILE)
                part = code[row, lane].astype(F32) * colinv[0:1, lane]
                total = part if total is None else total + part
            plane_msg[sweep, q, pl.ds(p, 1), :] = across_lanes(total)
            return carry

        lax.fori_loop(0, pairs, step, 0)

    def reduce_start(sweep):
        size = 2 * pairs if sweep == ITERS - 1 else pairs
        mine = plane_msg.at[sweep, q, pl.ds(0, size)]
        for step in range(1, plane):
            send(mine, mine, arp_send.at[sweep, step], arp_recv.at[sweep, step], plane_id(step))

    def reduce_middle(sweep):
        size = 2 * pairs if sweep == ITERS - 1 else pairs
        for step in range(1, plane):
            other = plane_msg.at[sweep, lax.rem(q - step + plane, plane), pl.ds(0, size)]
            arrive(other, arp_send.at[sweep, step], arp_recv.at[sweep, step], plane_id(step))
        total = plane_msg[sweep, 0, 0:size, :]
        for other in range(1, plane):
            total = total + plane_msg[sweep, other, 0:size, :]
        line_msg[sweep, z, 0:size, :] = total
        mine = line_msg.at[sweep, z, pl.ds(0, size)]
        for step in range(1, n_blk):
            send(mine, mine, arz_send.at[sweep, step], arz_recv.at[sweep, step], line_id(step))

    def reduce_end(sweep):
        size = 2 * pairs if sweep == ITERS - 1 else pairs
        for step in range(1, n_blk):
            other = line_msg.at[sweep, source(step), pl.ds(0, size)]
            arrive(other, arz_send.at[sweep, step], arz_recv.at[sweep, step], line_id(step))
        total = line_msg[sweep, 0, 0:size, :]
        for other in range(1, n_blk):
            total = total + line_msg[sweep, other, 0:size, :]
        rowinv[...] = 1.0 / total[0:pairs]
        if sweep == ITERS - 1:
            norminv[...] = (1.0 / SOFTMAX_TEMPER) / total[pairs:size]

    gather_a(0, rows_a, 0)
    load.wait()
    NC = min(256, cols)

    def normalize(t, carry):
        at = pl.ds(pl.multiple_of(t * NC, NC), NC)
        protos[at, :] = unit_rows(protos[at, :])
        return carry

    lax.fori_loop(0, cols // NC, normalize, 0)
    colacc[...] = jnp.zeros_like(colacc)
    gather_b(0, rows_a, 0)
    for k in range(n_blk):
        if k + 1 < n_blk:
            gather_a(0, rows_a, k + 1)
        if k == n_blk - 1:
            gather_a(1, rows_b, 0)
        gather_c(0, rows_a, k)
        code_group(k)
        if k + 1 < n_blk:
            gather_b(0, rows_a, k + 1)
    close_columns()
    for k in range(1, n_blk):
        gather_a(1, rows_b, k)
        gather_b(1, rows_b, k - 1)
    row_pass(0)
    reduce_start(0)
    gather_b(1, rows_b, n_blk - 1)
    for k in range(n_blk):
        gather_c(1, rows_b, k)

    share = [n_blk * i // 4 for i in range(5)]
    part = 0
    for sweep in range(ITERS):
        if sweep > 0:
            column_pass()
            row_pass(sweep)
            if sweep == ITERS - 1:
                plane_msg[sweep, q, pairs : 2 * pairs, :] = norminv[...]
            reduce_start(sweep)
        if sweep < 2:
            for zi in range(share[part], share[part + 1]):
                pred_group(zi)
            part += 1
        reduce_middle(sweep)
        if sweep < 2:
            for zi in range(share[part], share[part + 1]):
                pred_group(zi)
            part += 1
        reduce_end(sweep)

    def grad_group(zi, slot):
        def rows_step(t, carry):
            p = zi * n_dp + t
            row = pl.ds(pl.multiple_of(p * TILE, TILE), TILE)
            scale = down_rows(rowinv[pl.ds(p, 1), :] * (1.0 / SOFTMAX_TEMPER))
            weight = down_rows(norminv[pl.ds(p, 1), :])
            for j in range(tiles):
                lane = slice(j * TILE, (j + 1) * TILE)
                codes = (code[row, lane].astype(F32) * scale) * colinv[0:1, lane]
                code[row, lane] = (pred[row, lane] * weight - codes).astype(BF16)
            return carry

        lax.fori_loop(0, n_dp, rows_step, 0)

        def dot_step(t, carry):
            xs = t * PX
            size = PX * 2 * hit_dev
            row = pl.multiple_of(zi * group_rows + xs * 2 * hit_dev, size)
            part = jnp.dot(code[pl.ds(row, size), :], protos[...], preferred_element_type=F32)
            for i in range(PX):
                for core in range(2):
                    lo = (i * 2 + core) * hit_dev
                    hits2[slot, core, xs + i] = part[lo : lo + hit_dev, :]
            return carry

        lax.fori_loop(0, n_dp // PX, dot_step, 0)

    SLOTS = hits2.shape[0]
    order = list(range(1, n_blk)) + [0]
    sub_sends = {}
    dp_sends = {}

    def drain(copies):
        for old in copies:
            old.wait_send()
            sends[:] = [copy for copy in sends if copy is not old]

    def scatter_start(i):
        k = order[i]
        slot = i % SLOTS
        if i >= SLOTS:
            drain([sub_sends[i - SLOTS]])
        grad_group(lax.rem(z + k, n_blk), slot)
        sub_sends[i] = send(
            hits2.at[slot, 1 - c], s_in.at[k], rss_send.at[k], rss_recv.at[k], sub_id
        )

    def scatter_sub(i):
        k = order[i]
        slot = i % SLOTS
        arrive(s_in.at[k], rss_send.at[k], rss_recv.at[k], sub_id)
        if i >= SLOTS:
            drain(dp_sends[i - SLOTS])
        red[slot] = hits2[slot, c] + s_in[k]
        dp_sends[i] = []
        for dx in range(1, n_dp):
            other = lax.rem(x + dx, n_dp)
            dp_sends[i].append(
                send(
                    red.at[slot, other],
                    x_in.at[k, dx - 1],
                    rsx_send.at[k, dx],
                    rsx_recv.at[k, dx],
                    {"dp": other},
                )
            )

    def scatter_dp(i):
        k = order[i]
        total = red[i % SLOTS, x]
        for dx in range(1, n_dp):
            other = lax.rem(x + dx, n_dp)
            arrive(x_in.at[k, dx - 1], rsx_send.at[k, dx], rsx_recv.at[k, dx], {"dp": other})
            total = total + x_in[k, dx - 1]
        z_out[k] = total
        if k > 0:
            send(z_out.at[k], z_in.at[k], rsz_send.at[k], rsz_recv.at[k], line_id(k))

    def proto_cols(t, carry):
        lane = pl.ds(pl.multiple_of(t * CC, CC), CC)
        total = None
        for zi in range(n_blk):
            left = code[zi * group_rows : (zi + 1) * group_rows, lane]
            right = rows_b[zi].reshape(group_rows, width)
            part = lax.dot_general(
                left, right, (((0,), (0,)), ((), ())), preferred_element_type=F32
            )
            total = part if total is None else total + part
        gproto_ref[lane, :] = total
        return carry

    for i in range(n_blk):
        scatter_start(i)
        if i >= 1:
            scatter_sub(i - 1)
        if i >= 2:
            scatter_dp(i - 2)
    scatter_sub(n_blk - 1)
    chunks = cols // CC
    half = chunks // 2
    lax.fori_loop(0, half, proto_cols, 0)
    for i in range(max(0, n_blk - 2), n_blk):
        scatter_dp(i)
    lax.fori_loop(half, chunks, proto_cols, 0)
    total = z_out[0]
    for k in range(1, n_blk):
        arrive(z_in.at[k], rsz_send.at[k], rsz_recv.at[k], line_id(k))
        total = total + z_in[k]
    gview_ref[...] = total
    for copy in sends:
        copy.wait_send()


def body(view_a, view_b, prototypes, tile_mask, tile_region):
    n_blk = lax.axis_size("blk")
    n_dp = lax.axis_size("dp")
    hit_dev, width = view_a.shape
    plane = 2 * n_dp
    cols = prototypes.shape[0] // plane
    pairs = n_blk * n_dp
    hits = pairs * 2 * hit_dev
    slots = n_blk if n_blk <= 4 else 2
    dma = pltpu.SemaphoreType.DMA
    vmem = pl.BlockSpec(memory_space=pltpu.VMEM)
    smem = pl.BlockSpec(memory_space=pltpu.SMEM)
    return pl.pallas_call(
        functools.partial(kernel, n_blk, n_dp, hit_dev, cols),
        out_shape=(
            jax.ShapeDtypeStruct((hit_dev, width), F32),
            jax.ShapeDtypeStruct((cols, width), F32),
        ),
        in_specs=[smem, smem, vmem, vmem, pl.BlockSpec(memory_space=pl.ANY)],
        out_specs=(vmem, vmem),
        scratch_shapes=[
            pltpu.VMEM((n_blk, n_dp, 2, hit_dev, width), BF16),
            pltpu.VMEM((n_blk, n_dp, 2, hit_dev, width), BF16),
            pltpu.VMEM((cols, width), BF16),
            pltpu.VMEM((hits, cols), BF16),
            pltpu.VMEM((hits, cols), F32),
            pltpu.VMEM((min(2, n_dp) * 2 * hit_dev, TILE), F32),
            pltpu.VMEM((8, cols), F32),
            pltpu.VMEM((8, cols), F32),
            pltpu.VMEM((pairs, TILE), F32),
            pltpu.VMEM((pairs, TILE), F32),
            pltpu.VMEM((ITERS, plane, 2 * pairs, TILE), F32),
            pltpu.VMEM((ITERS, n_blk, 2 * pairs, TILE), F32),
            pltpu.VMEM((slots, 2, n_dp, hit_dev, width), F32),
            pltpu.VMEM((slots, n_dp, hit_dev, width), F32),
            pltpu.VMEM((n_blk, n_dp, hit_dev, width), F32),
            pltpu.VMEM((n_blk, n_dp - 1, hit_dev, width), F32),
            pltpu.VMEM((n_blk, hit_dev, width), F32),
            pltpu.VMEM((n_blk, hit_dev, width), F32),
            dma,
            dma((2, n_blk)),
            dma((2, n_blk)),
            dma((2, n_blk, n_dp)),
            dma((2, n_blk, n_dp)),
            dma((2, n_blk, n_dp)),
            dma((2, n_blk, n_dp)),
            dma((ITERS, plane)),
            dma((ITERS, plane)),
            dma((ITERS, n_blk)),
            dma((ITERS, n_blk)),
            dma((n_blk,)),
            dma((n_blk,)),
            dma((n_blk, n_dp)),
            dma((n_blk, n_dp)),
            dma((n_blk,)),
            dma((n_blk,)),
        ],
        compiler_params=pltpu.CompilerParams(
            collective_id=0, has_side_effects=True, vmem_limit_bytes=62 << 20
        ),
    )(tile_region, tile_mask, view_a, view_b, prototypes)


def solution(mesh):
    spread = P(("groups", "blk", "dp", "sub"), None)
    return jax.shard_map(
        body,
        mesh=mesh,
        in_specs=(spread, spread, P("blk", None), P(), P("groups")),
        out_specs=(spread, spread),
        check_vma=False,
    )
```

```python
import functools
import math

import jax
import jax.numpy as jnp
from jax import lax
from jax.experimental import pallas as pl
from jax.experimental.pallas import tpu as pltpu
from jax.sharding import PartitionSpec as P

TILE = 128
ITERS = 3
SOFTMAX_TEMPER = 0.1
EPSILON = 0.05
LOG2E = math.log2(math.e)
CODE_GAIN = LOG2E / EPSILON
PRED_GAIN = LOG2E / SOFTMAX_TEMPER
OFF = -1e30
MESH = pl.DeviceIdType.MESH
F32 = jnp.float32
BF16 = jnp.bfloat16


def unit_rows(matrix):
    values = matrix.astype(F32)
    return (values * lax.rsqrt(jnp.sum(values * values, axis=1, keepdims=True) + 1e-06)).astype(
        BF16
    )


def down_rows(row):
    return jnp.broadcast_to(row, (TILE, TILE)).T


def across_lanes(block):
    return jnp.sum(block.T, axis=0, keepdims=True)


def fold(block):
    return jnp.sum(block.reshape(block.shape[0] // 8, 8, block.shape[1]), axis=0)


def kernel(
    n_blk,
    n_dp,
    hit_dev,
    cols,
    region_ref,
    mask_ref,
    view_a_ref,
    view_b_ref,
    protos_ref,
    gview_ref,
    gproto_ref,
    rows_a,
    rows_b,
    protos,
    code,
    pred,
    lanes,
    colacc,
    colinv,
    rowinv,
    norminv,
    plane_msg,
    line_msg,
    hits2,
    red,
    s_in,
    x_in,
    z_out,
    z_in,
    load_sem,
    agz_send,
    agz_recv,
    agx_send,
    agx_recv,
    ags_send,
    ags_recv,
    arp_send,
    arp_recv,
    arz_send,
    arz_recv,
    rss_send,
    rss_recv,
    rsx_send,
    rsx_recv,
    rsz_send,
    rsz_recv,
):
    z = lax.axis_index("blk")
    x = lax.axis_index("dp")
    c = lax.axis_index("sub")
    plane = 2 * n_dp
    q = x * 2 + c
    group_rows = plane * hit_dev
    pairs = n_blk * n_dp
    tiles = cols // TILE
    first_tile = (z * plane + q) * tiles
    width = protos.shape[1]
    CC = min(1024, cols)
    ctiles = CC // TILE

    barrier = pltpu.get_barrier_semaphore()

    def plane_id(step):
        other = lax.rem(q + step, plane)
        return {"dp": lax.div(other, 2), "sub": lax.rem(other, 2)}

    def line_id(step):
        return {"blk": lax.rem(z + step, n_blk)}

    direct = n_blk * plane <= 16
    team = n_blk * plane if direct else plane
    me = z * plane + q if direct else q

    def team_id(step):
        if not direct:
            return plane_id(step)
        other = lax.rem(me + step, team)
        return {
            "blk": lax.div(other, plane),
            "dp": lax.rem(lax.div(other, 2), n_dp),
            "sub": lax.rem(other, 2),
        }

    for step in range(1, team):
        pl.semaphore_signal(barrier, inc=1, device_id=team_id(step), device_id_type=MESH)
    if not direct:
        for step in range(1, n_blk):
            pl.semaphore_signal(barrier, inc=1, device_id=line_id(step), device_id_type=MESH)

    load = pltpu.make_async_copy(protos_ref.at[pl.ds(q * cols, cols)], protos, load_sem)
    load.start()
    rows_a[z, x, c] = unit_rows(view_a_ref[...])
    rows_b[z, x, c] = unit_rows(view_b_ref[...])
    pl.semaphore_wait(barrier, team - 1 + (0 if direct else n_blk - 1))

    sends = []

    def send(src, dst, send_sem, recv_sem, device):
        copy = pltpu.make_async_remote_copy(
            src_ref=src,
            dst_ref=dst,
            send_sem=send_sem,
            recv_sem=recv_sem,
            device_id=device,
            device_id_type=MESH,
        )
        copy.start()
        sends.append(copy)
        return copy

    def arrive(dst, send_sem, recv_sem, device):
        pltpu.make_async_remote_copy(
            src_ref=dst,
            dst_ref=dst,
            send_sem=send_sem,
            recv_sem=recv_sem,
            device_id=device,
            device_id_type=MESH,
        ).wait_recv()

    sub_id = {"sub": 1 - c}

    def source(k):
        return lax.rem(z - k + n_blk, n_blk)

    def near(dx):
        return lax.rem(x - dx + n_dp, n_dp)

    def to_sub(v, rows, k, dx):
        ref = rows.at[source(k), near(dx), c]
        send(ref, ref, ags_send.at[v, k, dx], ags_recv.at[v, k, dx], sub_id)

    def gather_a(v, rows, k):
        ref = rows.at[source(k), x, c]
        if k == 0:
            for step in range(1, n_blk):
                send(ref, ref, agz_send.at[v, step], agz_recv.at[v, step], line_id(step))
        else:
            arrive(ref, agz_send.at[v, k], agz_recv.at[v, k], line_id(k))
        for dx in range(1, n_dp):
            send(
                ref,
                ref,
                agx_send.at[v, k, dx],
                agx_recv.at[v, k, dx],
                {"dp": lax.rem(x + dx, n_dp)},
            )
        to_sub(v, rows, k, 0)

    def gather_b(v, rows, k):
        for dx in range(1, n_dp):
            ref = rows.at[source(k), near(dx), c]
            arrive(
                ref,
                agx_send.at[v, k, dx],
                agx_recv.at[v, k, dx],
                {"dp": lax.rem(x + dx, n_dp)},
            )
            to_sub(v, rows, k, dx)

    def gather_c(v, rows, k):
        for dx in range(n_dp):
            ref = rows.at[source(k), near(dx), 1 - c]
            arrive(ref, ags_send.at[v, k, dx], ags_recv.at[v, k, dx], sub_id)

    def bias(pair, core, tile, gain):
        region = region_ref[pair * 2 + core]
        return jnp.where(mask_ref[region, first_tile + tile] > 0, -gain, OFF).astype(F32)

    def score(rows, zi, xs, count, col):
        left = rows[zi, pl.ds(xs, count)].reshape(count * 2 * hit_dev, width)
        right = protos[pl.ds(col, CC), :]
        return lax.dot_general(
            left, right, (((1,), (1,)), ((), ())), preferred_element_type=F32
        )

    PX = min(2, n_dp)

    def code_group(k):
        zi = source(k)

        def step(t, carry):
            xs = (t % (n_dp // PX)) * PX
            ci = t // (n_dp // PX)
            col = pl.multiple_of(ci * CC, CC)
            s = score(rows_a, zi, xs, PX, col)
            for j in range(ctiles):
                total = None
                lane = pl.ds(pl.multiple_of(col + j * TILE, TILE), TILE)
                for i in range(PX):
                    for core in range(2):
                        lo = (i * 2 + core) * hit_dev
                        piece = s[lo : lo + hit_dev, j * TILE : (j + 1) * TILE]
                        b = bias(zi * n_dp + xs + i, core, ci * ctiles + j, CODE_GAIN)
                        e = jnp.exp2(piece * CODE_GAIN + b).astype(BF16)
                        row = pl.multiple_of(zi * group_rows + xs * 2 * hit_dev + lo, hit_dev)
                        code[pl.ds(row, hit_dev), lane] = e
                        part = fold(e.astype(F32))
                        total = part if total is None else total + part
                colacc[:, lane] = colacc[:, lane] + total
            return carry

        lax.fori_loop(0, (n_dp // PX) * (cols // CC), step, 0)

    def pred_group(zi):
        def block(t, carry):
            xs = t * PX
            lanes[...] = jnp.zeros_like(lanes)

            def step(ci, inner):
                col = pl.multiple_of(ci * CC, CC)
                s = score(rows_b, zi, xs, PX, col)
                for i in range(PX):
                    for core in range(2):
                        lo = (i * 2 + core) * hit_dev
                        total = None
                        for j in range(ctiles):
                            piece = s[lo : lo + hit_dev, j * TILE : (j + 1) * TILE]
                            b = bias(zi * n_dp + xs + i, core, ci * ctiles + j, PRED_GAIN)
                            e = jnp.exp2(piece * PRED_GAIN + b)
                            row = pl.multiple_of(
                                zi * group_rows + xs * 2 * hit_dev + lo, hit_dev
                            )
                            lane = pl.ds(pl.multiple_of(col + j * TILE, TILE), TILE)
                            pred[pl.ds(row, hit_dev), lane] = e
                            total = e if total is None else total + e
                        lanes[lo : lo + hit_dev, :] = lanes[lo : lo + hit_dev, :] + total
                return inner

            lax.fori_loop(0, cols // CC, step, 0)
            for i in range(PX):
                norminv[pl.ds(zi * n_dp + xs + i, 1), :] = across_lanes(
                    lanes[i * TILE : (i + 1) * TILE, :]
                )
            return carry

        lax.fori_loop(0, n_dp // PX, block, 0)

    def close_columns():
        total = jnp.sum(colacc[...], axis=0, keepdims=True)
        colinv[...] = jnp.broadcast_to(1.0 / total, colinv.shape)

    def column_pass():
        colacc[...] = jnp.zeros_like(colacc)

        def step(p, carry):
            scale = down_rows(rowinv[pl.ds(p, 1), :])
            row = pl.ds(pl.multiple_of(p * TILE, TILE), TILE)
            for j in range(tiles):
                lane = slice(j * TILE, (j + 1) * TILE)
                colacc[:, lane] = colacc[:, lane] + fold(code[row, lane].astype(F32) * scale)
            return carry

        lax.fori_loop(0, pairs, step, 0)
        close_columns()

    def row_pass(sweep):
        def step(p, carry):
            row = pl.ds(pl.multiple_of(p * TILE, TILE), TILE)
            total = None
            for j in range(tiles):
                lane = slice(j * TILE, (j + 1) * TILE)
                part = code[row, lane].astype(F32) * colinv[0:1, lane]
                total = part if total is None else total + part
            plane_msg[sweep, me, pl.ds(p, 1), :] = across_lanes(total)
            return carry

        lax.fori_loop(0, pairs, step, 0)

    def reduce_start(sweep):
        size = 2 * pairs if sweep == ITERS - 1 else pairs
        mine = plane_msg.at[sweep, me, pl.ds(0, size)]
        for step in range(1, team):
            send(mine, mine, arp_send.at[sweep, step], arp_recv.at[sweep, step], team_id(step))

    def close_rows(sweep, total):
        rowinv[...] = 1.0 / total[0:pairs]
        if sweep == ITERS - 1:
            norminv[...] = (1.0 / SOFTMAX_TEMPER) / total[pairs : 2 * pairs]

    def reduce_middle(sweep):
        size = 2 * pairs if sweep == ITERS - 1 else pairs
        for step in range(1, team):
            other = plane_msg.at[sweep, lax.rem(me - step + team, team), pl.ds(0, size)]
            arrive(other, arp_send.at[sweep, step], arp_recv.at[sweep, step], team_id(step))
        total = plane_msg[sweep, 0, 0:size, :]
        for other in range(1, team):
            total = total + plane_msg[sweep, other, 0:size, :]
        if direct:
            close_rows(sweep, total)
            return
        line_msg[sweep, z, 0:size, :] = total
        mine = line_msg.at[sweep, z, pl.ds(0, size)]
        for step in range(1, n_blk):
            send(mine, mine, arz_send.at[sweep, step], arz_recv.at[sweep, step], line_id(step))

    def reduce_end(sweep):
        if direct:
            return
        size = 2 * pairs if sweep == ITERS - 1 else pairs
        for step in range(1, n_blk):
            other = line_msg.at[sweep, source(step), pl.ds(0, size)]
            arrive(other, arz_send.at[sweep, step], arz_recv.at[sweep, step], line_id(step))
        total = line_msg[sweep, 0, 0:size, :]
        for other in range(1, n_blk):
            total = total + line_msg[sweep, other, 0:size, :]
        close_rows(sweep, total)

    gather_a(0, rows_a, 0)
    load.wait()
    NC = min(256, cols)

    def normalize(t, carry):
        at = pl.ds(pl.multiple_of(t * NC, NC), NC)
        protos[at, :] = unit_rows(protos[at, :])
        return carry

    lax.fori_loop(0, cols // NC, normalize, 0)
    colacc[...] = jnp.zeros_like(colacc)
    gather_b(0, rows_a, 0)
    for k in range(n_blk):
        if k + 1 < n_blk:
            gather_a(0, rows_a, k + 1)
        if k == n_blk - 1:
            gather_a(1, rows_b, 0)
        gather_c(0, rows_a, k)
        code_group(k)
        if k + 1 < n_blk:
            gather_b(0, rows_a, k + 1)
    close_columns()
    for k in range(1, n_blk):
        gather_a(1, rows_b, k)
        gather_b(1, rows_b, k - 1)
    row_pass(0)
    reduce_start(0)
    gather_b(1, rows_b, n_blk - 1)
    for k in range(n_blk):
        gather_c(1, rows_b, k)

    share = [n_blk * i // 4 for i in range(5)]
    if direct:
        share = [0, n_blk // 2, n_blk // 2, n_blk, n_blk]
    part = 0
    for sweep in range(ITERS):
        if sweep > 0:
            column_pass()
            row_pass(sweep)
            if sweep == ITERS - 1:
                plane_msg[sweep, me, pairs : 2 * pairs, :] = norminv[...]
            reduce_start(sweep)
        if sweep < 2:
            for zi in range(share[part], share[part + 1]):
                pred_group(zi)
            part += 1
        reduce_middle(sweep)
        if sweep < 2:
            for zi in range(share[part], share[part + 1]):
                pred_group(zi)
            part += 1
        reduce_end(sweep)

    def grad_group(zi, slot):
        def rows_step(t, carry):
            p = zi * n_dp + t
            row = pl.ds(pl.multiple_of(p * TILE, TILE), TILE)
            scale = down_rows(rowinv[pl.ds(p, 1), :] * (1.0 / SOFTMAX_TEMPER))
            weight = down_rows(norminv[pl.ds(p, 1), :])
            for j in range(tiles):
                lane = slice(j * TILE, (j + 1) * TILE)
                codes = (code[row, lane].astype(F32) * scale) * colinv[0:1, lane]
                code[row, lane] = (pred[row, lane] * weight - codes).astype(BF16)
            return carry

        lax.fori_loop(0, n_dp, rows_step, 0)

        def dot_step(t, carry):
            xs = t * PX
            size = PX * 2 * hit_dev
            row = pl.multiple_of(zi * group_rows + xs * 2 * hit_dev, size)
            part = jnp.dot(code[pl.ds(row, size), :], protos[...], preferred_element_type=F32)
            for i in range(PX):
                for core in range(2):
                    lo = (i * 2 + core) * hit_dev
                    hits2[slot, core, xs + i] = part[lo : lo + hit_dev, :]
            return carry

        lax.fori_loop(0, n_dp // PX, dot_step, 0)

    SLOTS = hits2.shape[0]
    order = list(range(1, n_blk)) + [0]
    sub_sends = {}
    dp_sends = {}

    def drain(copies):
        for old in copies:
            old.wait_send()
            sends[:] = [copy for copy in sends if copy is not old]

    def scatter_start(i):
        k = order[i]
        slot = i % SLOTS
        if i >= SLOTS:
            drain([sub_sends[i - SLOTS]])
        grad_group(lax.rem(z + k, n_blk), slot)
        sub_sends[i] = send(
            hits2.at[slot, 1 - c], s_in.at[k], rss_send.at[k], rss_recv.at[k], sub_id
        )

    def scatter_sub(i):
        k = order[i]
        slot = i % SLOTS
        arrive(s_in.at[k], rss_send.at[k], rss_recv.at[k], sub_id)
        if i >= SLOTS:
            drain(dp_sends[i - SLOTS])
        red[slot] = hits2[slot, c] + s_in[k]
        dp_sends[i] = []
        for dx in range(1, n_dp):
            other = lax.rem(x + dx, n_dp)
            dp_sends[i].append(
                send(
                    red.at[slot, other],
                    x_in.at[k, dx - 1],
                    rsx_send.at[k, dx],
                    rsx_recv.at[k, dx],
                    {"dp": other},
                )
            )

    def scatter_dp(i):
        k = order[i]
        total = red[i % SLOTS, x]
        for dx in range(1, n_dp):
            other = lax.rem(x + dx, n_dp)
            arrive(x_in.at[k, dx - 1], rsx_send.at[k, dx], rsx_recv.at[k, dx], {"dp": other})
            total = total + x_in[k, dx - 1]
        z_out[k] = total
        if k > 0:
            send(z_out.at[k], z_in.at[k], rsz_send.at[k], rsz_recv.at[k], line_id(k))

    def proto_cols(t, carry):
        lane = pl.ds(pl.multiple_of(t * CC, CC), CC)
        total = None
        for zi in range(n_blk):
            left = code[zi * group_rows : (zi + 1) * group_rows, lane]
            right = rows_b[zi].reshape(group_rows, width)
            part = lax.dot_general(
                left, right, (((0,), (0,)), ((), ())), preferred_element_type=F32
            )
            total = part if total is None else total + part
        gproto_ref[lane, :] = total
        return carry

    for i in range(n_blk):
        scatter_start(i)
        if i >= 1:
            scatter_sub(i - 1)
        if i >= 2:
            scatter_dp(i - 2)
    scatter_sub(n_blk - 1)
    chunks = cols // CC
    half = chunks // 2
    lax.fori_loop(0, half, proto_cols, 0)
    for i in range(max(0, n_blk - 2), n_blk):
        scatter_dp(i)
    lax.fori_loop(half, chunks, proto_cols, 0)
    total = z_out[0]
    for k in range(1, n_blk):
        arrive(z_in.at[k], rsz_send.at[k], rsz_recv.at[k], line_id(k))
        total = total + z_in[k]
    gview_ref[...] = total
    for copy in sends:
        copy.wait_send()


def body(view_a, view_b, prototypes, tile_mask, tile_region):
    n_blk = lax.axis_size("blk")
    n_dp = lax.axis_size("dp")
    hit_dev, width = view_a.shape
    plane = 2 * n_dp
    cols = prototypes.shape[0] // plane
    pairs = n_blk * n_dp
    hits = pairs * 2 * hit_dev
    team = n_blk * plane if n_blk * plane <= 16 else plane
    slots = n_blk if n_blk <= 4 else 2
    dma = pltpu.SemaphoreType.DMA
    vmem = pl.BlockSpec(memory_space=pltpu.VMEM)
    smem = pl.BlockSpec(memory_space=pltpu.SMEM)
    return pl.pallas_call(
        functools.partial(kernel, n_blk, n_dp, hit_dev, cols),
        out_shape=(
            jax.ShapeDtypeStruct((hit_dev, width), F32),
            jax.ShapeDtypeStruct((cols, width), F32),
        ),
        in_specs=[smem, smem, vmem, vmem, pl.BlockSpec(memory_space=pl.ANY)],
        out_specs=(vmem, vmem),
        scratch_shapes=[
            pltpu.VMEM((n_blk, n_dp, 2, hit_dev, width), BF16),
            pltpu.VMEM((n_blk, n_dp, 2, hit_dev, width), BF16),
            pltpu.VMEM((cols, width), BF16),
            pltpu.VMEM((hits, cols), BF16),
            pltpu.VMEM((hits, cols), F32),
            pltpu.VMEM((min(2, n_dp) * 2 * hit_dev, TILE), F32),
            pltpu.VMEM((8, cols), F32),
            pltpu.VMEM((8, cols), F32),
            pltpu.VMEM((pairs, TILE), F32),
            pltpu.VMEM((pairs, TILE), F32),
            pltpu.VMEM((ITERS, team, 2 * pairs, TILE), F32),
            pltpu.VMEM((ITERS, n_blk, 2 * pairs, TILE), F32),
            pltpu.VMEM((slots, 2, n_dp, hit_dev, width), F32),
            pltpu.VMEM((slots, n_dp, hit_dev, width), F32),
            pltpu.VMEM((n_blk, n_dp, hit_dev, width), F32),
            pltpu.VMEM((n_blk, n_dp - 1, hit_dev, width), F32),
            pltpu.VMEM((n_blk, hit_dev, width), F32),
            pltpu.VMEM((n_blk, hit_dev, width), F32),
            dma,
            dma((2, n_blk)),
            dma((2, n_blk)),
            dma((2, n_blk, n_dp)),
            dma((2, n_blk, n_dp)),
            dma((2, n_blk, n_dp)),
            dma((2, n_blk, n_dp)),
            dma((ITERS, team)),
            dma((ITERS, team)),
            dma((ITERS, n_blk)),
            dma((ITERS, n_blk)),
            dma((n_blk,)),
            dma((n_blk,)),
            dma((n_blk, n_dp)),
            dma((n_blk, n_dp)),
            dma((n_blk,)),
            dma((n_blk,)),
        ],
        compiler_params=pltpu.CompilerParams(
            collective_id=0, has_side_effects=True, vmem_limit_bytes=(50 if team > plane else 62) << 20
        ),
    )(tile_region, tile_mask, view_a, view_b, prototypes)


def solution(mesh):
    spread = P(("groups", "blk", "dp", "sub"), None)
    return jax.shard_map(
        body,
        mesh=mesh,
        in_specs=(spread, spread, P("blk", None), P(), P("groups")),
        out_specs=(spread, spread),
        check_vma=False,
    )
```

```python
import functools
import math

import jax
import jax.numpy as jnp
from jax import lax
from jax.experimental import pallas as pl
from jax.experimental.pallas import tpu as pltpu
from jax.sharding import PartitionSpec as P

TILE = 128
ITERS = 3
SOFTMAX_TEMPER = 0.1
EPSILON = 0.05
LOG2E = math.log2(math.e)
CODE_GAIN = LOG2E / EPSILON
PRED_GAIN = LOG2E / SOFTMAX_TEMPER
OFF = -1e30
MESH = pl.DeviceIdType.MESH
F32 = jnp.float32
BF16 = jnp.bfloat16


def unit_rows(matrix):
    values = matrix.astype(F32)
    return (values * lax.rsqrt(jnp.sum(values * values, axis=1, keepdims=True) + 1e-06)).astype(
        BF16
    )


def down_rows(row):
    return jnp.broadcast_to(row, (TILE, TILE)).T


def across_lanes(block):
    return jnp.sum(block.T, axis=0, keepdims=True)


def fold(block):
    return jnp.sum(block.reshape(block.shape[0] // 8, 8, block.shape[1]), axis=0)


def kernel(
    n_blk,
    n_dp,
    hit_dev,
    cols,
    region_ref,
    mask_ref,
    view_a_ref,
    view_b_ref,
    protos_ref,
    gview_ref,
    gproto_ref,
    rows_a,
    rows_b,
    protos,
    code,
    pred,
    lanes,
    colacc,
    colinv,
    rowinv,
    norminv,
    plane_msg,
    line_msg,
    hits2,
    red,
    s_in,
    x_in,
    z_out,
    z_in,
    load_sem,
    agz_send,
    agz_recv,
    agx_send,
    agx_recv,
    ags_send,
    ags_recv,
    arp_send,
    arp_recv,
    arz_send,
    arz_recv,
    rss_send,
    rss_recv,
    rsx_send,
    rsx_recv,
    rsz_send,
    rsz_recv,
):
    z = lax.axis_index("blk")
    x = lax.axis_index("dp")
    c = lax.axis_index("sub")
    plane = 2 * n_dp
    q = x * 2 + c
    group_rows = plane * hit_dev
    pairs = n_blk * n_dp
    tiles = cols // TILE
    first_tile = (z * plane + q) * tiles
    width = protos.shape[1]
    CC = min(1024, cols)
    ctiles = CC // TILE

    barrier = pltpu.get_barrier_semaphore()

    def plane_id(step):
        other = lax.rem(q + step, plane)
        return {"dp": lax.div(other, 2), "sub": lax.rem(other, 2)}

    def line_id(step):
        return {"blk": lax.rem(z + step, n_blk)}

    direct = n_blk * plane <= 16
    team = n_blk * plane if direct else plane
    me = z * plane + q if direct else q

    def team_id(step):
        if not direct:
            return plane_id(step)
        other = lax.rem(me + step, team)
        return {
            "blk": lax.div(other, plane),
            "dp": lax.rem(lax.div(other, 2), n_dp),
            "sub": lax.rem(other, 2),
        }

    for step in range(1, team):
        pl.semaphore_signal(barrier, inc=1, device_id=team_id(step), device_id_type=MESH)
    if not direct:
        for step in range(1, n_blk):
            pl.semaphore_signal(barrier, inc=1, device_id=line_id(step), device_id_type=MESH)

    load = pltpu.make_async_copy(protos_ref.at[pl.ds(q * cols, cols)], protos, load_sem)
    load.start()
    rows_a[z, x, c] = unit_rows(view_a_ref[...])
    rows_b[z, x, c] = unit_rows(view_b_ref[...])
    pl.semaphore_wait(barrier, team - 1 + (0 if direct else n_blk - 1))

    sends = []

    def send(src, dst, send_sem, recv_sem, device):
        copy = pltpu.make_async_remote_copy(
            src_ref=src,
            dst_ref=dst,
            send_sem=send_sem,
            recv_sem=recv_sem,
            device_id=device,
            device_id_type=MESH,
        )
        copy.start()
        sends.append(copy)
        return copy

    def arrive(dst, send_sem, recv_sem, device):
        pltpu.make_async_remote_copy(
            src_ref=dst,
            dst_ref=dst,
            send_sem=send_sem,
            recv_sem=recv_sem,
            device_id=device,
            device_id_type=MESH,
        ).wait_recv()

    sub_id = {"sub": 1 - c}

    def source(k):
        return lax.rem(z - k + n_blk, n_blk)

    def near(dx):
        return lax.rem(x - dx + n_dp, n_dp)

    def to_sub(v, rows, k, dx):
        ref = rows.at[source(k), near(dx), c]
        send(ref, ref, ags_send.at[v, k, dx], ags_recv.at[v, k, dx], sub_id)

    def gather_a(v, rows, k):
        ref = rows.at[source(k), x, c]
        if k == 0:
            for step in range(1, n_blk):
                send(ref, ref, agz_send.at[v, step], agz_recv.at[v, step], line_id(step))
        else:
            arrive(ref, agz_send.at[v, k], agz_recv.at[v, k], line_id(k))
        for dx in range(1, n_dp):
            send(
                ref,
                ref,
                agx_send.at[v, k, dx],
                agx_recv.at[v, k, dx],
                {"dp": lax.rem(x + dx, n_dp)},
            )
        to_sub(v, rows, k, 0)

    def gather_b(v, rows, k):
        for dx in range(1, n_dp):
            ref = rows.at[source(k), near(dx), c]
            arrive(
                ref,
                agx_send.at[v, k, dx],
                agx_recv.at[v, k, dx],
                {"dp": lax.rem(x + dx, n_dp)},
            )
            to_sub(v, rows, k, dx)

    def gather_c(v, rows, k):
        for dx in range(n_dp):
            ref = rows.at[source(k), near(dx), 1 - c]
            arrive(ref, ags_send.at[v, k, dx], ags_recv.at[v, k, dx], sub_id)

    def bias(pair, core, tile, gain):
        region = region_ref[pair * 2 + core]
        return jnp.where(mask_ref[region, first_tile + tile] > 0, -gain, OFF).astype(F32)

    def score(rows, zi, xs, count, col):
        left = rows[zi, pl.ds(xs, count)].reshape(count * 2 * hit_dev, width)
        right = protos[pl.ds(col, CC), :]
        return lax.dot_general(
            left, right, (((1,), (1,)), ((), ())), preferred_element_type=F32
        )

    PX = min(2, n_dp)

    def code_group(k):
        zi = source(k)

        def step(t, carry):
            xs = (t % (n_dp // PX)) * PX
            ci = t // (n_dp // PX)
            col = pl.multiple_of(ci * CC, CC)
            s = score(rows_a, zi, xs, PX, col)
            for j in range(ctiles):
                total = None
                lane = pl.ds(pl.multiple_of(col + j * TILE, TILE), TILE)
                for i in range(PX):
                    for core in range(2):
                        lo = (i * 2 + core) * hit_dev
                        piece = s[lo : lo + hit_dev, j * TILE : (j + 1) * TILE]
                        b = bias(zi * n_dp + xs + i, core, ci * ctiles + j, CODE_GAIN)
                        e = jnp.exp2(piece * CODE_GAIN + b).astype(BF16)
                        row = pl.multiple_of(zi * group_rows + xs * 2 * hit_dev + lo, hit_dev)
                        code[pl.ds(row, hit_dev), lane] = e
                        part = fold(e.astype(F32))
                        total = part if total is None else total + part
                colacc[:, lane] = colacc[:, lane] + total
            return carry

        lax.fori_loop(0, (n_dp // PX) * (cols // CC), step, 0)

    def pred_group(zi):
        def block(t, carry):
            xs = t * PX
            lanes[...] = jnp.zeros_like(lanes)

            def step(ci, inner):
                col = pl.multiple_of(ci * CC, CC)
                s = score(rows_b, zi, xs, PX, col)
                for i in range(PX):
                    for core in range(2):
                        lo = (i * 2 + core) * hit_dev
                        total = None
                        for j in range(ctiles):
                            piece = s[lo : lo + hit_dev, j * TILE : (j + 1) * TILE]
                            b = bias(zi * n_dp + xs + i, core, ci * ctiles + j, PRED_GAIN)
                            e = jnp.exp2(piece * PRED_GAIN + b)
                            row = pl.multiple_of(
                                zi * group_rows + xs * 2 * hit_dev + lo, hit_dev
                            )
                            lane = pl.ds(pl.multiple_of(col + j * TILE, TILE), TILE)
                            pred[pl.ds(row, hit_dev), lane] = e
                            total = e if total is None else total + e
                        lanes[lo : lo + hit_dev, :] = lanes[lo : lo + hit_dev, :] + total
                return inner

            lax.fori_loop(0, cols // CC, step, 0)
            for i in range(PX):
                norminv[pl.ds(zi * n_dp + xs + i, 1), :] = across_lanes(
                    lanes[i * TILE : (i + 1) * TILE, :]
                )
            return carry

        lax.fori_loop(0, n_dp // PX, block, 0)

    def close_columns():
        total = jnp.sum(colacc[...], axis=0, keepdims=True)
        colinv[...] = jnp.broadcast_to(1.0 / total, colinv.shape)

    def column_pass():
        colacc[...] = jnp.zeros_like(colacc)

        def step(p, carry):
            scale = down_rows(rowinv[pl.ds(p, 1), :])
            row = pl.ds(pl.multiple_of(p * TILE, TILE), TILE)
            for j in range(tiles):
                lane = slice(j * TILE, (j + 1) * TILE)
                colacc[:, lane] = colacc[:, lane] + fold(code[row, lane].astype(F32) * scale)
            return carry

        lax.fori_loop(0, pairs, step, 0)
        close_columns()

    def row_pass(sweep):
        def step(p, carry):
            row = pl.ds(pl.multiple_of(p * TILE, TILE), TILE)
            total = None
            for j in range(tiles):
                lane = slice(j * TILE, (j + 1) * TILE)
                part = code[row, lane].astype(F32) * colinv[0:1, lane]
                total = part if total is None else total + part
            plane_msg[sweep, me, pl.ds(p, 1), :] = across_lanes(total)
            return carry

        lax.fori_loop(0, pairs, step, 0)

    def reduce_start(sweep):
        size = 2 * pairs if sweep == ITERS - 1 else pairs
        mine = plane_msg.at[sweep, me, pl.ds(0, size)]
        for step in range(1, team):
            send(mine, mine, arp_send.at[sweep, step], arp_recv.at[sweep, step], team_id(step))

    def close_rows(sweep, total):
        rowinv[...] = 1.0 / total[0:pairs]
        if sweep == ITERS - 1:
            norminv[...] = (1.0 / SOFTMAX_TEMPER) / total[pairs : 2 * pairs]

    def reduce_middle(sweep):
        size = 2 * pairs if sweep == ITERS - 1 else pairs
        for step in range(1, team):
            other = plane_msg.at[sweep, lax.rem(me - step + team, team), pl.ds(0, size)]
            arrive(other, arp_send.at[sweep, step], arp_recv.at[sweep, step], team_id(step))
        total = plane_msg[sweep, 0, 0:size, :]
        for other in range(1, team):
            total = total + plane_msg[sweep, other, 0:size, :]
        if direct:
            close_rows(sweep, total)
            return
        line_msg[sweep, z, 0:size, :] = total
        mine = line_msg.at[sweep, z, pl.ds(0, size)]
        for step in range(1, n_blk):
            send(mine, mine, arz_send.at[sweep, step], arz_recv.at[sweep, step], line_id(step))

    def reduce_end(sweep):
        if direct:
            return
        size = 2 * pairs if sweep == ITERS - 1 else pairs
        for step in range(1, n_blk):
            other = line_msg.at[sweep, source(step), pl.ds(0, size)]
            arrive(other, arz_send.at[sweep, step], arz_recv.at[sweep, step], line_id(step))
        total = line_msg[sweep, 0, 0:size, :]
        for other in range(1, n_blk):
            total = total + line_msg[sweep, other, 0:size, :]
        close_rows(sweep, total)

    gather_a(0, rows_a, 0)
    load.wait()
    NC = min(256, cols)

    def normalize(t, carry):
        at = pl.ds(pl.multiple_of(t * NC, NC), NC)
        protos[at, :] = unit_rows(protos[at, :])
        return carry

    lax.fori_loop(0, cols // NC, normalize, 0)
    colacc[...] = jnp.zeros_like(colacc)
    gather_b(0, rows_a, 0)
    for k in range(n_blk):
        if k + 1 < n_blk:
            gather_a(0, rows_a, k + 1)
        if k == n_blk - 1:
            gather_a(1, rows_b, 0)
        gather_c(0, rows_a, k)
        code_group(k)
        if k + 1 < n_blk:
            gather_b(0, rows_a, k + 1)
    close_columns()
    for k in range(1, n_blk):
        gather_a(1, rows_b, k)
        gather_b(1, rows_b, k - 1)
    row_pass(0)
    reduce_start(0)
    gather_b(1, rows_b, n_blk - 1)
    for k in range(n_blk):
        gather_c(1, rows_b, k)

    share = [n_blk * i // 4 for i in range(5)]
    if direct:
        share = [0, n_blk // 2, n_blk // 2, n_blk, n_blk]
    part = 0
    for sweep in range(ITERS):
        if sweep > 0:
            column_pass()
            row_pass(sweep)
            if sweep == ITERS - 1:
                plane_msg[sweep, me, pairs : 2 * pairs, :] = norminv[...]
            reduce_start(sweep)
        if sweep < 2:
            for zi in range(share[part], share[part + 1]):
                pred_group(zi)
            part += 1
        reduce_middle(sweep)
        if sweep < 2:
            for zi in range(share[part], share[part + 1]):
                pred_group(zi)
            part += 1
        reduce_end(sweep)

    def grad_group(zi, slot):
        def rows_step(t, carry):
            p = zi * n_dp + t
            row = pl.ds(pl.multiple_of(p * TILE, TILE), TILE)
            scale = down_rows(rowinv[pl.ds(p, 1), :] * (1.0 / SOFTMAX_TEMPER))
            weight = down_rows(norminv[pl.ds(p, 1), :])
            for j in range(tiles):
                lane = slice(j * TILE, (j + 1) * TILE)
                codes = (code[row, lane].astype(F32) * scale) * colinv[0:1, lane]
                code[row, lane] = (pred[row, lane] * weight - codes).astype(BF16)
            return carry

        lax.fori_loop(0, n_dp, rows_step, 0)

        def dot_step(t, carry):
            xs = t * PX
            size = PX * 2 * hit_dev
            row = pl.multiple_of(zi * group_rows + xs * 2 * hit_dev, size)
            part = jnp.dot(code[pl.ds(row, size), :], protos[...], preferred_element_type=F32)
            for i in range(PX):
                for core in range(2):
                    lo = (i * 2 + core) * hit_dev
                    hits2[slot, core, xs + i] = part[lo : lo + hit_dev, :]
            return carry

        lax.fori_loop(0, n_dp // PX, dot_step, 0)

    SLOTS = hits2.shape[0]
    order = list(range(1, n_blk)) + [0]
    sub_sends = {}
    dp_sends = {}

    def drain(copies):
        for old in copies:
            old.wait_send()
            sends[:] = [copy for copy in sends if copy is not old]

    def scatter_start(i):
        k = order[i]
        slot = i % SLOTS
        if i >= SLOTS:
            drain([sub_sends[i - SLOTS]])
        grad_group(lax.rem(z + k, n_blk), slot)
        sub_sends[i] = send(
            hits2.at[slot, 1 - c], s_in.at[k], rss_send.at[k], rss_recv.at[k], sub_id
        )

    def scatter_sub(i):
        k = order[i]
        slot = i % SLOTS
        arrive(s_in.at[k], rss_send.at[k], rss_recv.at[k], sub_id)
        if i >= SLOTS:
            drain(dp_sends[i - SLOTS])
        red[slot] = hits2[slot, c] + s_in[k]
        dp_sends[i] = []
        for dx in range(1, n_dp):
            other = lax.rem(x + dx, n_dp)
            dp_sends[i].append(
                send(
                    red.at[slot, other],
                    x_in.at[k, dx - 1],
                    rsx_send.at[k, dx],
                    rsx_recv.at[k, dx],
                    {"dp": other},
                )
            )

    def scatter_dp(i):
        k = order[i]
        total = red[i % SLOTS, x]
        for dx in range(1, n_dp):
            other = lax.rem(x + dx, n_dp)
            arrive(x_in.at[k, dx - 1], rsx_send.at[k, dx], rsx_recv.at[k, dx], {"dp": other})
            total = total + x_in[k, dx - 1]
        z_out[k] = total
        if k > 0:
            send(z_out.at[k], z_in.at[k], rsz_send.at[k], rsz_recv.at[k], line_id(k))

    PC = min(512, cols)

    def proto_cols(t, carry):
        lane = pl.ds(pl.multiple_of(t * PC, PC), PC)
        total = None
        for zi in range(n_blk):
            left = code[zi * group_rows : (zi + 1) * group_rows, lane]
            right = rows_b[zi].reshape(group_rows, width)
            part = lax.dot_general(
                left, right, (((0,), (0,)), ((), ())), preferred_element_type=F32
            )
            total = part if total is None else total + part
        gproto_ref[lane, :] = total
        return carry

    for i in range(n_blk):
        scatter_start(i)
        if i >= 1:
            scatter_sub(i - 1)
        if i >= 2:
            scatter_dp(i - 2)
    chunks = cols // PC
    cut = [chunks * i // 4 for i in range(5)]
    lax.fori_loop(cut[0], cut[1], proto_cols, 0)
    scatter_sub(n_blk - 1)
    if n_blk >= 2:
        scatter_dp(n_blk - 2)
    lax.fori_loop(cut[1], cut[2], proto_cols, 0)
    scatter_dp(n_blk - 1)
    lax.fori_loop(cut[2], cut[4], proto_cols, 0)
    total = z_out[0]
    for k in range(1, n_blk):
        arrive(z_in.at[k], rsz_send.at[k], rsz_recv.at[k], line_id(k))
        total = total + z_in[k]
    gview_ref[...] = total
    for copy in sends:
        copy.wait_send()


def body(view_a, view_b, prototypes, tile_mask, tile_region):
    n_blk = lax.axis_size("blk")
    n_dp = lax.axis_size("dp")
    hit_dev, width = view_a.shape
    plane = 2 * n_dp
    cols = prototypes.shape[0] // plane
    pairs = n_blk * n_dp
    hits = pairs * 2 * hit_dev
    team = n_blk * plane if n_blk * plane <= 16 else plane
    slots = n_blk if n_blk <= 4 else 2
    dma = pltpu.SemaphoreType.DMA
    vmem = pl.BlockSpec(memory_space=pltpu.VMEM)
    smem = pl.BlockSpec(memory_space=pltpu.SMEM)
    return pl.pallas_call(
        functools.partial(kernel, n_blk, n_dp, hit_dev, cols),
        out_shape=(
            jax.ShapeDtypeStruct((hit_dev, width), F32),
            jax.ShapeDtypeStruct((cols, width), F32),
        ),
        in_specs=[smem, smem, vmem, vmem, pl.BlockSpec(memory_space=pl.ANY)],
        out_specs=(vmem, vmem),
        scratch_shapes=[
            pltpu.VMEM((n_blk, n_dp, 2, hit_dev, width), BF16),
            pltpu.VMEM((n_blk, n_dp, 2, hit_dev, width), BF16),
            pltpu.VMEM((cols, width), BF16),
            pltpu.VMEM((hits, cols), BF16),
            pltpu.VMEM((hits, cols), F32),
            pltpu.VMEM((min(2, n_dp) * 2 * hit_dev, TILE), F32),
            pltpu.VMEM((8, cols), F32),
            pltpu.VMEM((8, cols), F32),
            pltpu.VMEM((pairs, TILE), F32),
            pltpu.VMEM((pairs, TILE), F32),
            pltpu.VMEM((ITERS, team, 2 * pairs, TILE), F32),
            pltpu.VMEM((ITERS, n_blk, 2 * pairs, TILE), F32),
            pltpu.VMEM((slots, 2, n_dp, hit_dev, width), F32),
            pltpu.VMEM((slots, n_dp, hit_dev, width), F32),
            pltpu.VMEM((n_blk, n_dp, hit_dev, width), F32),
            pltpu.VMEM((n_blk, n_dp - 1, hit_dev, width), F32),
            pltpu.VMEM((n_blk, hit_dev, width), F32),
            pltpu.VMEM((n_blk, hit_dev, width), F32),
            dma,
            dma((2, n_blk)),
            dma((2, n_blk)),
            dma((2, n_blk, n_dp)),
            dma((2, n_blk, n_dp)),
            dma((2, n_blk, n_dp)),
            dma((2, n_blk, n_dp)),
            dma((ITERS, team)),
            dma((ITERS, team)),
            dma((ITERS, n_blk)),
            dma((ITERS, n_blk)),
            dma((n_blk,)),
            dma((n_blk,)),
            dma((n_blk, n_dp)),
            dma((n_blk, n_dp)),
            dma((n_blk,)),
            dma((n_blk,)),
        ],
        compiler_params=pltpu.CompilerParams(
            collective_id=0, has_side_effects=True, vmem_limit_bytes=(50 if team > plane else 62) << 20
        ),
    )(tile_region, tile_mask, view_a, view_b, prototypes)


def solution(mesh):
    spread = P(("groups", "blk", "dp", "sub"), None)
    return jax.shard_map(
        body,
        mesh=mesh,
        in_specs=(spread, spread, P("blk", None), P(), P("groups")),
        out_specs=(spread, spread),
        check_vma=False,
    )
```
